32 devices in a mesh: survey: 2 (over y), gz: 4 (over z), gy: 2 (over x), pat: 2 (over core).
Axes of the slice: x: 2, y: 2, z: 4, core: 2. Of those that a mesh axis runs over, the one named last changes fastest.
Arguments:
- conductivity: float32 [32, 256, 512], P(('survey', 'gz'), 'gy'), parts along dimension 0, may hold values from 0.3 to 3
- receivers: int32 [4, 3, 64], P(('survey', 'pat')), parts along dimension 0, may hold values from 0 to 511, as said below
- observed: float32 [4, 64], P(('survey', 'pat')), parts along dimension 0, may hold values from -6 to 6
- potential: float32 [2, 32, 256, 512], P('pat', ('survey', 'gz'), 'gy'), parts along dimension 1, may hold values from -6 to 6
- adjoint_prev: float32 [2, 32, 256, 512], P('pat', ('survey', 'gz'), 'gy'), parts along dimension 1, may hold values from -0.046875 to 0.046875
Outputs:
- adjoint: float32 [2, 32, 256, 512], P('pat', ('survey', 'gz'), 'gy'), parts along dimension 1
- gradient: float32 [32, 256, 512], P(('survey', 'gz'), 'gy'), parts along dimension 0
The draws below stay inside these ranges and needn't reach their ends.
There are 2 independent parts, one for each index of `survey`. The reference program is written for one: setup_inputs(seed, part) draws one part's arguments, and reference() takes and returns one part's arrays. A program takes and returns all parts, laid end to end along the dimension named above; each array names one. Nothing has to cross between parts.
Inputs may be any that keep to these rules, and one draw needn't show every extreme that they name: receivers[p, 0, r], receivers[p, 1, r] and receivers[p, 2, r] are a z cell below 16, a y cell below 256 and an x cell below 512; several receivers may share a cell.
All inputs are finite; a program needn't handle non-finite values.
Results may differ from the reference program's by a relative error of at most 0.0003.
Values sent between devices are 32-bit elements; how exact they have to be, the bound alone decides.
A program may use at most 64 MiB of HBM per device.

```python
import math
import jax
import jax.numpy as jnp
from jax import lax

NX = 512
RECV = 64
SWEEPS = 2
NZ = 16
NY = 256
PATTERNS = 2


def draw_receivers(key, part):
    key_z, key_y, key_x = jax.random.split(jax.random.fold_in(key, 11), 3)
    z_cell = jax.random.randint(key_z, (PATTERNS, 1, RECV), 0, NZ)
    y_cell = jax.random.randint(key_y, (PATTERNS, 1, RECV), 0, NY)
    x_cell = jax.random.randint(key_x, (PATTERNS, 1, RECV), 0, NX)
    return jnp.concatenate([z_cell, y_cell, x_cell], axis=1).astype(jnp.int32)


def block_scale(key, shape, cuts, smallest, largest):
    gain = 1.0
    for dim, blocks in cuts:
        draws = jax.random.uniform(jax.random.fold_in(jax.random.fold_in(key, 6), dim), (blocks,), jnp.float32, smallest / len(cuts), largest / len(cuts))
        gain = gain * jnp.repeat(jnp.exp(draws), shape[dim] // blocks).reshape((-1,) + (1,) * (len(shape) - 1 - dim))
    return gain


def normal_values(stream_key, shape, spread, bound, pieces=(), kind=jnp.bfloat16):
    gain = block_scale(stream_key, shape, pieces, -0.22, 0.18) if pieces else 1.0
    entries = jax.random.normal(stream_key, shape, jnp.float32) * spread * gain
    return jnp.minimum(jnp.maximum(entries, -bound), bound).astype(kind)


def setup_inputs(seed: int = 0, part: int = 0) -> dict:
    splits = jax.random.split(jax.random.key(seed), 6)
    part_splits = jax.random.split(jax.random.fold_in(splits[5], part), 6)
    conductivity = jnp.clip(jnp.exp(math.log(3.0) - 2.3025851 * jax.random.uniform(part_splits[0], (NZ, NY, NX), jnp.float32) ** block_scale(part_splits[0], (NZ, NY, NX), ((0, 4), (1, 2)), -0.2, 0.2)), 0.3, 3.0)
    receivers = draw_receivers(jax.random.fold_in(jax.random.fold_in(splits[5], part), 71), part)
    observed = normal_values(part_splits[2], (PATTERNS, RECV), 1.5, 6.0, ((0, 2),), jnp.float32)
    potential = normal_values(part_splits[3], (PATTERNS, NZ, NY, NX), 1.0, 6.0, ((0, 2), (1, 4), (2, 2)), jnp.float32)
    adjoint_prev = normal_values(part_splits[4], (PATTERNS, NZ, NY, NX), 0.003, 0.046875, ((0, 2), (1, 4), (2, 2)), jnp.float32)
    return {"conductivity": conductivity, "receivers": receivers, "observed": observed, "potential": potential, "adjoint_prev": adjoint_prev}


relax_weight = 0.8


def beside_cells(extended):
    widened = jnp.pad(extended, [(0, 0)] * (extended.ndim - 1) + [(1, 1)])
    centre = widened[..., 1:-1, 1:-1, 1:-1]
    others = [widened[..., 2:, 1:-1, 1:-1], widened[..., :-2, 1:-1, 1:-1],
              widened[..., 1:-1, 2:, 1:-1], widened[..., 1:-1, :-2, 1:-1],
              widened[..., 1:-1, 1:-1, 2:], widened[..., 1:-1, 1:-1, :-2]]
    return centre, others


def pad_rim(field):
    return jnp.pad(field, [(0, 0)] * (field.ndim - 3) + [(1, 1), (1, 1), (0, 0)])


def relax(cond_ext, adjoint_ext, source):
    cond_mid, cond_near = beside_cells(cond_ext)
    adj_mid, adj_near = beside_cells(adjoint_ext)
    diagonal = jnp.zeros_like(cond_mid)
    coupled = jnp.zeros_like(adj_mid)
    for cond_side, adj_side in zip(cond_near, adj_near):
        face_coef = 0.5 * (cond_mid + cond_side)
        diagonal = diagonal + face_coef
        coupled = coupled + face_coef * adj_side
    return adj_mid + relax_weight * (source - diagonal * adj_mid + coupled) / diagonal


def contribution(pot_ext, adj_ext):
    pot_mid, pot_near = beside_cells(pot_ext)
    adj_mid, adj_near = beside_cells(adj_ext)
    summed = jnp.zeros_like(adj_mid)
    for pot_side, adj_side in zip(pot_near, adj_near):
        summed = summed + (pot_mid - pot_side) * (adj_mid - adj_side)
    return -0.5 * jnp.sum(summed, axis=0)


def receiver_source(field, receivers, observed, z_start, y_start):
    z_count = field.shape[1]
    y_count = field.shape[2]
    z_local = receivers[:, 0, :] - z_start
    y_local = receivers[:, 1, :] - y_start
    x_local = receivers[:, 2, :]
    inside = (z_local >= 0) & (z_local < z_count) & (y_local >= 0) & (y_local < y_count)
    z_local = jnp.clip(z_local, 0, z_count - 1).astype(jnp.int32)
    y_local = jnp.clip(y_local, 0, y_count - 1).astype(jnp.int32)
    pattern_ids = jnp.broadcast_to(jnp.arange(field.shape[0], dtype=jnp.int32)[:, None], z_local.shape)
    values = jnp.where(inside, field[pattern_ids, z_local, y_local, x_local] - observed, jnp.zeros_like(observed))
    return jnp.zeros_like(field).at[pattern_ids, z_local, y_local, x_local].add(values)


def reference(conductivity, receivers, observed, potential, adjoint_prev):
    cond_ext = pad_rim(conductivity)

    def one_pattern(inputs):
        pot_one, adj_one, recv_one, obs_one = inputs
        pot_one = pot_one[None]
        source = receiver_source(pot_one, recv_one[None], obs_one[None], 0, 0)
        field = adj_one[None]
        for sweep_index in range(SWEEPS):
            field = relax(cond_ext, pad_rim(field), source)
        return field[0], contribution(pad_rim(pot_one), pad_rim(field))

    adjoint, terms = lax.map(one_pattern, (potential, adjoint_prev, receivers, observed))
    return adjoint, jnp.sum(terms, axis=0)
```

```python
import functools

import jax
import jax.numpy as jnp
from jax import lax
from jax.experimental import pallas as pl
from jax.experimental.pallas import tpu as pltpu
from jax.sharding import PartitionSpec as P

relax_weight = 0.8
MESH = pl.DeviceIdType.MESH
PAD = 8
CHUNKS = 4
COND, ADJ0, POT, ADJ1, ADJ2 = range(5)
UP, DOWN = 0, 1
HIGH = lax.Precision.HIGHEST


def kernel(
    counts,
    cond_hbm,
    recv_ref,
    obs_ref,
    pot_hbm,
    adj_hbm,
    adj_out,
    grad_out,
    cond,
    adj0,
    pot,
    adj1,
    adj2,
    source,
    weight,
    grad,
    grad_far,
    load_sem,
    out_sem,
    z_send,
    z_recv,
    y_send,
    y_recv,
    relay_send,
    relay_recv,
    g_send,
    g_recv,
):
    gz_count, gy_count = counts
    planes, rows, lanes = cond_hbm.shape
    top = planes + 1
    chunk = rows // CHUNKS
    half = rows // 2
    gz = lax.axis_index("gz")
    gy = lax.axis_index("gy")
    pat = lax.axis_index("pat")
    partner = 1 - pat
    z_has = (gz < gz_count - 1, gz > 0)
    z_from = (gz > 0, gz < gz_count - 1)
    z_to = ({"gz": gz + 1}, {"gz": gz - 1})
    y_has = (gy < gy_count - 1, gy > 0)
    y_from = (gy > 0, gy < gy_count - 1)
    y_to = ({"gy": gy + 1}, {"gy": gy - 1})
    inside = pl.ds(PAD, rows)

    hbm_of = {COND: cond_hbm, ADJ0: adj_hbm.at[0], POT: pot_hbm.at[0]}
    vmem_of = {COND: cond, ADJ0: adj0, POT: pot, ADJ1: adj1, ADJ2: adj2}

    loads = []
    for field in (COND, ADJ0, POT):
        loads.append(
            pltpu.make_async_copy(
                hbm_of[field], vmem_of[field].at[pl.ds(1, planes), inside], load_sem.at[field]
            )
        )
    for copy in loads:
        copy.start()

    barrier = pltpu.get_barrier_semaphore()
    for way in (UP, DOWN):

        @pl.when(z_has[way])
        def _():
            pl.semaphore_signal(barrier, inc=1, device_id=z_to[way], device_id_type=MESH)

        @pl.when(y_has[way])
        def _():
            pl.semaphore_signal(barrier, inc=1, device_id=y_to[way], device_id_type=MESH)

    pl.semaphore_signal(barrier, inc=1, device_id={"pat": partner}, device_id_type=MESH)

    for field in range(5):
        buf = vmem_of[field]
        for way in (UP, DOWN):

            @pl.when(jnp.logical_not(z_from[way]))
            def _():
                buf[0 if way == UP else top, PAD : PAD + rows] = jnp.zeros((rows, lanes), jnp.float32)

            @pl.when(jnp.logical_not(y_from[way]))
            def _():
                at = 0 if way == UP else PAD + rows
                buf[1:top, at : at + PAD] = jnp.zeros((planes, PAD, lanes), jnp.float32)

    neighbours = (
        1
        + z_has[0].astype(jnp.int32)
        + z_has[1].astype(jnp.int32)
        + y_has[0].astype(jnp.int32)
        + y_has[1].astype(jnp.int32)
    )
    pl.semaphore_wait(barrier, neighbours)

    def z_copy(field, way, part):
        buf = vmem_of[field]
        ghost = 0 if way == UP else top
        if field == COND:
            start, count = pl.multiple_of(pat * half, 8), half
        else:
            start, count = part * chunk, chunk
        if field in hbm_of:
            src = hbm_of[field].at[planes - 1 if way == UP else 0, pl.ds(start, count)]
        else:
            src = buf.at[planes if way == UP else 1, pl.ds(PAD + start, count)]
        return pltpu.make_async_remote_copy(
            src_ref=src,
            dst_ref=buf.at[ghost, pl.ds(PAD + start, count)],
            send_sem=z_send.at[field, way, part],
            recv_sem=z_recv.at[field, way, part],
            device_id=z_to[way],
            device_id_type=MESH,
        )

    def y_copy(field, way):
        buf = vmem_of[field]
        ghost = 0 if way == UP else PAD + rows
        if field in hbm_of:
            src = hbm_of[field].at[:, pl.ds(rows - PAD if way == UP else 0, PAD)]
        else:
            src = buf.at[pl.ds(1, planes), pl.ds(rows if way == UP else PAD, PAD)]
        return pltpu.make_async_remote_copy(
            src_ref=src,
            dst_ref=buf.at[pl.ds(1, planes), pl.ds(ghost, PAD)],
            send_sem=y_send.at[field, way],
            recv_sem=y_recv.at[field, way],
            device_id=y_to[way],
            device_id_type=MESH,
        )

    def relay(way):
        at = cond.at[0 if way == UP else top, pl.ds(pl.multiple_of(PAD + pat * half, 8), half)]
        return pltpu.make_async_remote_copy(
            src_ref=at,
            dst_ref=at,
            send_sem=relay_send.at[way],
            recv_sem=relay_recv.at[way],
            device_id={"pat": partner},
            device_id_type=MESH,
        )

    def g_copy(part):
        plane = part // CHUNKS
        at = pl.ds((part % CHUNKS) * chunk, chunk)
        return pltpu.make_async_remote_copy(
            src_ref=grad.at[plane, at],
            dst_ref=grad_far.at[plane, at],
            send_sem=g_send.at[part],
            recv_sem=g_recv.at[part],
            device_id={"pat": partner},
            device_id_type=MESH,
        )

    def guarded(flag, action):
        @pl.when(flag)
        def _():
            action()

    def start_z(field, way, part):
        guarded(z_has[way], lambda: z_copy(field, way, part).start())

    def wait_z(field, way, part):
        guarded(z_from[way], lambda: z_copy(field, way, part).wait_recv())

    def start_y(field):
        for way in (UP, DOWN):
            guarded(y_has[way], lambda: y_copy(field, way).start())

    def wait_y(field):
        for way in (UP, DOWN):
            guarded(y_from[way], lambda: y_copy(field, way).wait_recv())

    for way in (UP, DOWN):
        start_z(COND, way, 0)
    for part in range(CHUNKS):
        for way in (UP, DOWN):
            start_z(ADJ0, way, part)
    for field in (COND, ADJ0, POT):
        start_y(field)

    for copy in loads:
        copy.wait()

    recv_count = recv_ref.shape[-1]
    z_at = recv_ref[0, 0:1, :] - gz * planes
    y_at = recv_ref[0, 1:2, :] - gy * rows
    near = (z_at >= 0) & (z_at < planes) & (y_at >= 0) & (y_at < rows)
    line = jnp.where(near, z_at * rows + y_at, -1)
    eye = lax.broadcasted_iota(jnp.int32, (recv_count, recv_count), 0) == lax.broadcasted_iota(
        jnp.int32, (recv_count, recv_count), 1
    )

    def column(row):
        wide = jnp.broadcast_to(row.astype(jnp.float32), (recv_count, recv_count))
        return jnp.sum(jnp.where(eye, wide, 0.0), axis=1, keepdims=True)

    line_col = column(line).astype(jnp.int32)
    x_col = column(recv_ref[0, 2:3, :]).astype(jnp.int32)
    obs_col = column(obs_ref[...])
    picked = jnp.zeros((recv_count, lanes), jnp.float32)
    along = lax.broadcasted_iota(jnp.int32, (recv_count, rows), 1)
    for plane in range(planes):
        hot = jnp.where(along + plane * rows == line_col, 1.0, 0.0)
        picked = picked + jnp.dot(
            hot, pot[plane + 1, PAD : PAD + rows], precision=HIGH, preferred_element_type=jnp.float32
        )
    at_x = lax.broadcasted_iota(jnp.int32, (recv_count, lanes), 1) == x_col
    value = jnp.sum(jnp.where(at_x, picked, 0.0), axis=1, keepdims=True) - obs_col
    value = jnp.where(line_col >= 0, value, 0.0)
    spread = jnp.where(at_x, jnp.broadcast_to(value, at_x.shape), 0.0)
    down_rows = lax.broadcasted_iota(jnp.int32, (rows, recv_count), 0)
    for plane in range(planes):
        hot = jnp.where(down_rows + plane * rows == line, 1.0, 0.0)
        source[plane] = jnp.dot(hot, spread, precision=HIGH, preferred_element_type=jnp.float32)

    lane = lax.broadcasted_iota(jnp.int32, (8, lanes), 1)
    at_left = lane == 0
    at_right = lane == lanes - 1

    def left_of(v):
        return jnp.where(at_left, 0.0, pltpu.roll(v, 1, 1))

    def right_of(v):
        return jnp.where(at_right, 0.0, pltpu.roll(v, lanes - 1, 1))

    sub = lax.broadcasted_iota(jnp.int32, (8, lanes), 0)

    def beside(buf, plane, r, middle):
        before = buf[plane, pl.ds(pl.multiple_of(r - 8, 8), 8)]
        after = buf[plane, pl.ds(pl.multiple_of(r + 8, 8), 8)]
        return (
            pltpu.roll(jnp.where(sub == 7, before, middle), 1, 0),
            pltpu.roll(jnp.where(sub == 0, after, middle), 7, 0),
            buf[plane - 1, pl.ds(r, 8)],
            buf[plane + 1, pl.ds(r, 8)],
        )

    def relax_block(old, new, plane, r, first):
        c = cond[plane, pl.ds(r, 8)]
        a = old[plane, pl.ds(r, 8)]
        q = c * a
        sum_a = left_of(a) + right_of(a)
        sum_q = left_of(q) + right_of(q)
        if first:
            sum_c = left_of(c) + right_of(c)
        for c_n, a_n in zip(beside(cond, plane, r, c), beside(old, plane, r, a)):
            sum_a = sum_a + a_n
            sum_q = sum_q + c_n * a_n
            if first:
                sum_c = sum_c + c_n
        if first:
            diag = 3.0 * c + 0.5 * sum_c
            w = relax_weight / diag
            weight[plane - 1, pl.ds(pl.multiple_of(r - PAD, 8), 8)] = w
        else:
            w = weight[plane - 1, pl.ds(pl.multiple_of(r - PAD, 8), 8)]
        s = source[plane - 1, pl.ds(pl.multiple_of(r - PAD, 8), 8)]
        coupled = 0.5 * (c * sum_a + sum_q)
        new[plane, pl.ds(r, 8)] = (1.0 - relax_weight) * a + w * (s + coupled)

    def grad_block(plane, r):
        p = pot[plane, pl.ds(r, 8)]
        a = adj2[plane, pl.ds(r, 8)]
        total = (p - left_of(p)) * (a - left_of(a)) + (p - right_of(p)) * (a - right_of(a))
        for p_n, a_n in zip(beside(pot, plane, r, p), beside(adj2, plane, r, a)):
            total = total + (p - p_n) * (a - a_n)
        grad[plane - 1, pl.ds(pl.multiple_of(r - PAD, 8), 8)] = -0.5 * total

    def over_rows(first_row, count, action):
        def body(i, carry):
            action(pl.multiple_of(PAD + first_row + i * 8, 8))
            return carry

        lax.fori_loop(0, count // 8, body, 0)

    inner = list(range(2, planes))
    edges = [(1, UP), (planes, DOWN)]

    wait_y(COND)
    wait_y(ADJ0)
    for plane in inner:
        over_rows(0, rows, lambda r: relax_block(adj0, adj1, plane, r, True))
    for way in (UP, DOWN):

        def pass_on():
            z_copy(COND, way, 0).wait_recv()
            relay(way).start()

        guarded(z_from[way], pass_on)
    for way in (UP, DOWN):
        guarded(z_from[way], lambda: relay(way).wait())
    for part in range(CHUNKS):
        for plane, way in edges:
            wait_z(ADJ0, way, part)
            over_rows(part * chunk, chunk, lambda r: relax_block(adj0, adj1, plane, r, True))
            start_z(ADJ1, 1 - way, part)
    start_y(ADJ1)
    for part in range(CHUNKS):
        for way in (UP, DOWN):
            start_z(POT, way, part)

    wait_y(ADJ1)
    for plane in inner:
        over_rows(0, rows, lambda r: relax_block(adj1, adj2, plane, r, False))
    for part in range(CHUNKS):
        for plane, way in edges:
            wait_z(ADJ1, way, part)
            over_rows(part * chunk, chunk, lambda r: relax_block(adj1, adj2, plane, r, False))
            start_z(ADJ2, 1 - way, part)
    start_y(ADJ2)
    adj_store = pltpu.make_async_copy(
        adj2.at[pl.ds(1, planes), inside], adj_out.at[0], out_sem.at[0]
    )
    adj_store.start()

    wait_y(POT)
    wait_y(ADJ2)
    sent = []
    for plane in inner:
        over_rows(0, rows, lambda r: grad_block(plane, r))
        for part in range(CHUNKS):
            sent.append((plane - 1) * CHUNKS + part)
            g_copy(sent[-1]).start()
    for part in range(CHUNKS):
        for plane, way in edges:
            wait_z(POT, way, part)
            wait_z(ADJ2, way, part)
            over_rows(part * chunk, chunk, lambda r: grad_block(plane, r))
            sent.append((plane - 1) * CHUNKS + part)
            g_copy(sent[-1]).start()
    stores = []
    for part in sent:
        plane, start = part // CHUNKS, (part % CHUNKS) * chunk
        at = pl.ds(start, chunk)
        g_copy(part).wait_recv()
        grad_far[plane, at] = grad_far[plane, at] + grad[plane, at]
        stores.append(
            pltpu.make_async_copy(
                grad_far.at[plane, at], grad_out.at[plane, at], out_sem.at[1 + part]
            )
        )
        stores[-1].start()

    for part in sent:
        g_copy(part).wait_send()
    for way in (UP, DOWN):

        def z_done():
            z_copy(COND, way, 0).wait_send()
            for field in (ADJ0, POT, ADJ1, ADJ2):
                for part in range(CHUNKS):
                    z_copy(field, way, part).wait_send()

        def y_done():
            for field in range(5):
                y_copy(field, way).wait_send()

        guarded(z_has[way], z_done)
        guarded(y_has[way], y_done)
    adj_store.wait()
    for store in stores:
        store.wait()


def local(counts, conductivity, receivers, observed, potential, adjoint_prev):
    planes, rows, lanes = conductivity.shape
    wide = pltpu.VMEM((planes + 2, rows + 2 * PAD, lanes), jnp.float32)
    body = pltpu.VMEM((planes, rows, lanes), jnp.float32)
    dma = pltpu.SemaphoreType.DMA
    anywhere = pl.BlockSpec(memory_space=pl.ANY)
    in_vmem = pl.BlockSpec(memory_space=pltpu.VMEM)
    return pl.pallas_call(
        functools.partial(kernel, counts),
        out_shape=(
            jax.ShapeDtypeStruct(adjoint_prev.shape, jnp.float32),
            jax.ShapeDtypeStruct(conductivity.shape, jnp.float32),
        ),
        in_specs=[anywhere, in_vmem, in_vmem, anywhere, anywhere],
        out_specs=(anywhere, anywhere),
        scratch_shapes=[wide] * 5
        + [body] * 4
        + [
            dma((3,)),
            dma((1 + planes * CHUNKS,)),
            dma((5, 2, CHUNKS)),
            dma((5, 2, CHUNKS)),
            dma((5, 2)),
            dma((5, 2)),
            dma((2,)),
            dma((2,)),
            dma((planes * CHUNKS,)),
            dma((planes * CHUNKS,)),
        ],
        compiler_params=pltpu.CompilerParams(
            collective_id=0, has_side_effects=True, vmem_limit_bytes=40 * 1024 * 1024
        ),
    )(conductivity, receivers, observed, potential, adjoint_prev)


def solution(mesh):
    counts = (mesh.shape["gz"], mesh.shape["gy"])
    return jax.shard_map(
        functools.partial(local, counts),
        mesh=mesh,
        in_specs=(
            P(("survey", "gz"), "gy", None),
            P(("survey", "pat"), None, None),
            P(("survey", "pat"), None),
            P("pat", ("survey", "gz"), "gy", None),
            P("pat", ("survey", "gz"), "gy", None),
        ),
        out_specs=(P("pat", ("survey", "gz"), "gy", None), P(("survey", "gz"), "gy", None)),
        check_vma=False,
    )
```

```python
import functools

import jax
import jax.numpy as jnp
from jax import lax
from jax.experimental import pallas as pl
from jax.experimental.pallas import tpu as pltpu
from jax.sharding import PartitionSpec as P

relax_weight = 0.8
MESH = pl.DeviceIdType.MESH
PAD = 8
UNROLLS = (4, 2, 1)
VMEM_LIMIT = 32 * 1024 * 1024
CHUNKS = 4
COND, ADJ0, POT, ADJ1, ADJ2 = range(5)
UP, DOWN = 0, 1
HIGH = lax.Precision.HIGHEST


def kernel(
    counts,
    cond_hbm,
    recv_hbm,
    obs_hbm,
    pot_hbm,
    adj_hbm,
    adj_out,
    grad,
    grad_far,
    cond,
    adj0,
    pot,
    adj1,
    adj2,
    source,
    weight,
    recv_ref,
    obs_ref,
    load_sem,
    z_send,
    z_recv,
    y_send,
    y_recv,
    relay_send,
    relay_recv,
    g_send,
    g_recv,
):
    gz_count, gy_count = counts
    planes, rows, lanes = cond_hbm.shape
    top = planes + 1
    chunk = rows // CHUNKS
    half = rows // 2
    gz = lax.axis_index("gz")
    gy = lax.axis_index("gy")
    pat = lax.axis_index("pat")
    partner = 1 - pat
    z_has = (gz < gz_count - 1, gz > 0)
    z_from = (gz > 0, gz < gz_count - 1)
    z_to = ({"gz": gz + 1}, {"gz": gz - 1})
    y_has = (gy < gy_count - 1, gy > 0)
    y_from = (gy > 0, gy < gy_count - 1)
    y_to = ({"gy": gy + 1}, {"gy": gy - 1})
    inside = pl.ds(PAD, rows)

    hbm_of = {COND: cond_hbm, ADJ0: adj_hbm.at[0], POT: pot_hbm.at[0]}
    vmem_of = {COND: cond, ADJ0: adj0, POT: pot, ADJ1: adj1, ADJ2: adj2}

    loads = []
    for field in (COND, ADJ0, POT):
        loads.append(
            pltpu.make_async_copy(
                hbm_of[field], vmem_of[field].at[pl.ds(1, planes), inside], load_sem.at[field]
            )
        )
    loads.append(pltpu.make_async_copy(recv_hbm, recv_ref, load_sem.at[3]))
    loads.append(pltpu.make_async_copy(obs_hbm, obs_ref, load_sem.at[4]))
    for copy in loads:
        copy.start()

    barrier = pltpu.get_barrier_semaphore()
    for way in (UP, DOWN):

        @pl.when(z_has[way])
        def _():
            pl.semaphore_signal(barrier, inc=1, device_id=z_to[way], device_id_type=MESH)

        @pl.when(y_has[way])
        def _():
            pl.semaphore_signal(barrier, inc=1, device_id=y_to[way], device_id_type=MESH)

    pl.semaphore_signal(barrier, inc=1, device_id={"pat": partner}, device_id_type=MESH)

    for field in range(5):
        buf = vmem_of[field]
        for way in (UP, DOWN):

            @pl.when(jnp.logical_not(z_from[way]))
            def _():
                buf[0 if way == UP else top, PAD : PAD + rows] = jnp.zeros((rows, lanes), jnp.float32)

            @pl.when(jnp.logical_not(y_from[way]))
            def _():
                at = 0 if way == UP else PAD + rows
                buf[1:top, at : at + PAD] = jnp.zeros((planes, PAD, lanes), jnp.float32)

    neighbours = (
        1
        + z_has[0].astype(jnp.int32)
        + z_has[1].astype(jnp.int32)
        + y_has[0].astype(jnp.int32)
        + y_has[1].astype(jnp.int32)
    )
    pl.semaphore_wait(barrier, neighbours)

    def z_copy(field, way, part):
        buf = vmem_of[field]
        ghost = 0 if way == UP else top
        if field == COND:
            start, count = pl.multiple_of(pat * half, 8), half
        else:
            start, count = part * chunk, chunk
        if field in hbm_of:
            src = hbm_of[field].at[planes - 1 if way == UP else 0, pl.ds(start, count)]
        else:
            src = buf.at[planes if way == UP else 1, pl.ds(PAD + start, count)]
        return pltpu.make_async_remote_copy(
            src_ref=src,
            dst_ref=buf.at[ghost, pl.ds(PAD + start, count)],
            send_sem=z_send.at[field, way, part],
            recv_sem=z_recv.at[field, way, part],
            device_id=z_to[way],
            device_id_type=MESH,
        )

    def y_copy(field, way):
        buf = vmem_of[field]
        ghost = 0 if way == UP else PAD + rows
        if field in hbm_of:
            src = hbm_of[field].at[:, pl.ds(rows - PAD if way == UP else 0, PAD)]
        else:
            src = buf.at[pl.ds(1, planes), pl.ds(rows if way == UP else PAD, PAD)]
        return pltpu.make_async_remote_copy(
            src_ref=src,
            dst_ref=buf.at[pl.ds(1, planes), pl.ds(ghost, PAD)],
            send_sem=y_send.at[field, way],
            recv_sem=y_recv.at[field, way],
            device_id=y_to[way],
            device_id_type=MESH,
        )

    def relay(way):
        at = cond.at[0 if way == UP else top, pl.ds(pl.multiple_of(PAD + pat * half, 8), half)]
        return pltpu.make_async_remote_copy(
            src_ref=at,
            dst_ref=at,
            send_sem=relay_send.at[way],
            recv_sem=relay_recv.at[way],
            device_id={"pat": partner},
            device_id_type=MESH,
        )

    def g_copy(part):
        plane = part // CHUNKS
        at = pl.ds((part % CHUNKS) * chunk, chunk)
        return pltpu.make_async_remote_copy(
            src_ref=grad.at[plane, at],
            dst_ref=grad_far.at[plane, at],
            send_sem=g_send.at[part],
            recv_sem=g_recv.at[part],
            device_id={"pat": partner},
            device_id_type=MESH,
        )

    def guarded(flag, action):
        @pl.when(flag)
        def _():
            action()

    def start_z(field, way, part):
        guarded(z_has[way], lambda: z_copy(field, way, part).start())

    def wait_z(field, way, part):
        guarded(z_from[way], lambda: z_copy(field, way, part).wait_recv())

    def start_y(field):
        for way in (UP, DOWN):
            guarded(y_has[way], lambda: y_copy(field, way).start())

    def wait_y(field):
        for way in (UP, DOWN):
            guarded(y_from[way], lambda: y_copy(field, way).wait_recv())

    for way in (UP, DOWN):
        start_z(COND, way, 0)
    for part in [0] + ([CHUNKS - 1] if CHUNKS > 1 else []) + list(range(1, CHUNKS - 1)):
        for way in (UP, DOWN):
            start_z(ADJ0, way, part)
    for field in (COND, ADJ0, POT):
        start_y(field)

    for copy in loads:
        copy.wait()

    recv_count = recv_ref.shape[-1]
    z_at = recv_ref[0] - gz * planes
    y_at = recv_ref[1] - gy * rows
    near = (z_at >= 0) & (z_at < planes) & (y_at >= 0) & (y_at < rows)
    line = jnp.where(near, z_at * rows + y_at, -1)
    eye = lax.broadcasted_iota(jnp.int32, (recv_count, recv_count), 0) == lax.broadcasted_iota(
        jnp.int32, (recv_count, recv_count), 1
    )

    def column(row):
        wide = jnp.broadcast_to(row.astype(jnp.float32), (recv_count, recv_count))
        return jnp.sum(jnp.where(eye, wide, 0.0), axis=1, keepdims=True)

    line_col = column(line).astype(jnp.int32)
    x_col = column(recv_ref[2]).astype(jnp.int32)
    obs_col = column(obs_ref[...])
    picked = jnp.zeros((recv_count, lanes), jnp.float32)
    along = lax.broadcasted_iota(jnp.int32, (recv_count, rows), 1)
    for plane in range(planes):
        hot = jnp.where(along + plane * rows == line_col, 1.0, 0.0)
        picked = picked + jnp.dot(
            hot, pot[plane + 1, PAD : PAD + rows], precision=HIGH, preferred_element_type=jnp.float32
        )
    at_x = lax.broadcasted_iota(jnp.int32, (recv_count, lanes), 1) == x_col
    value = jnp.sum(jnp.where(at_x, picked, 0.0), axis=1, keepdims=True) - obs_col
    value = jnp.where(line_col >= 0, value, 0.0)
    spread = jnp.where(at_x, jnp.broadcast_to(value, at_x.shape), 0.0)
    down_rows = lax.broadcasted_iota(jnp.int32, (rows, recv_count), 0)
    for plane in range(planes):
        hot = jnp.where(down_rows + plane * rows == line, 1.0, 0.0)
        source[plane] = jnp.dot(hot, spread, precision=HIGH, preferred_element_type=jnp.float32)

    lane = lax.broadcasted_iota(jnp.int32, (8, lanes), 1)
    at_left = lane == 0
    at_right = lane == lanes - 1

    def left_of(v):
        return jnp.where(at_left, 0.0, pltpu.roll(v, 1, 1))

    def right_of(v):
        return jnp.where(at_right, 0.0, pltpu.roll(v, lanes - 1, 1))

    sub = lax.broadcasted_iota(jnp.int32, (8, lanes), 0)

    def beside(buf, plane, r, middle):
        before = buf[plane, pl.ds(pl.multiple_of(r - 8, 8), 8)]
        after = buf[plane, pl.ds(pl.multiple_of(r + 8, 8), 8)]
        return (
            pltpu.roll(jnp.where(sub == 7, before, middle), 1, 0),
            pltpu.roll(jnp.where(sub == 0, after, middle), 7, 0),
            buf[plane - 1, pl.ds(r, 8)],
            buf[plane + 1, pl.ds(r, 8)],
        )

    def relax_block(old, new, plane, r, first):
        c = cond[plane, pl.ds(r, 8)]
        a = old[plane, pl.ds(r, 8)]
        q = c * a
        sum_a = left_of(a) + right_of(a)
        sum_q = left_of(q) + right_of(q)
        if first:
            sum_c = left_of(c) + right_of(c)
        for c_n, a_n in zip(beside(cond, plane, r, c), beside(old, plane, r, a)):
            sum_a = sum_a + a_n
            sum_q = sum_q + c_n * a_n
            if first:
                sum_c = sum_c + c_n
        if first:
            diag = 3.0 * c + 0.5 * sum_c
            w = relax_weight / diag
            weight[plane - 1, pl.ds(pl.multiple_of(r - PAD, 8), 8)] = w
        else:
            w = weight[plane - 1, pl.ds(pl.multiple_of(r - PAD, 8), 8)]
        s = source[plane - 1, pl.ds(pl.multiple_of(r - PAD, 8), 8)]
        coupled = 0.5 * (c * sum_a + sum_q)
        value = (1.0 - relax_weight) * a + w * (s + coupled)
        new[plane, pl.ds(r, 8)] = value
        if not first:
            adj_out[0, plane - 1, pl.ds(pl.multiple_of(r - PAD, 8), 8)] = value

    def grad_block(plane, r):
        p = pot[plane, pl.ds(r, 8)]
        a = adj2[plane, pl.ds(r, 8)]
        total = (p - left_of(p)) * (a - left_of(a)) + (p - right_of(p)) * (a - right_of(a))
        for p_n, a_n in zip(beside(pot, plane, r, p), beside(adj2, plane, r, a)):
            total = total + (p - p_n) * (a - a_n)
        grad[plane - 1, pl.ds(pl.multiple_of(r - PAD, 8), 8)] = -0.5 * total

    def over_rows(first_row, count, action):
        blocks = count // 8
        step = next(n for n in UNROLLS if blocks % n == 0)

        def body(i, carry):
            for k in range(step):
                action(pl.multiple_of(PAD + first_row + (i * step + k) * 8, 8))
            return carry

        lax.fori_loop(0, blocks // step, body, 0)

    inner = list(range(2, planes))
    edges = [(1, UP), (planes, DOWN)]

    parts = [0] + ([CHUNKS - 1] if CHUNKS > 1 else []) + list(range(1, CHUNKS - 1))
    rims = [0, rows - 8]

    def sweep_inner(action, field):
        for plane in inner:
            over_rows(8, rows - 16, lambda r: action(plane, r))
        for each in field:
            wait_y(each)
        for plane in inner:
            for r in rims:
                action(plane, PAD + r)

    def first_block(plane, r):
        relax_block(adj0, adj1, plane, r, True)

    def second_block(plane, r):
        relax_block(adj1, adj2, plane, r, False)

    sweep_inner(first_block, (COND, ADJ0))
    for way in (UP, DOWN):

        def pass_on():
            z_copy(COND, way, 0).wait_recv()
            relay(way).start()

        guarded(z_from[way], pass_on)
    for way in (UP, DOWN):
        guarded(z_from[way], lambda: relay(way).wait())
    for i, part in enumerate(parts):
        for plane, way in edges:
            wait_z(ADJ0, way, part)
            over_rows(part * chunk, chunk, lambda r: first_block(plane, r))
            start_z(ADJ1, 1 - way, part)
        if i == min(1, CHUNKS - 1):
            start_y(ADJ1)
    for part in parts:
        for way in (UP, DOWN):
            start_z(POT, way, part)

    sweep_inner(second_block, (ADJ1,))
    for i, part in enumerate(parts):
        for plane, way in edges:
            wait_z(ADJ1, way, part)
            over_rows(part * chunk, chunk, lambda r: second_block(plane, r))
            start_z(ADJ2, 1 - way, part)
        if i == min(1, CHUNKS - 1):
            start_y(ADJ2)

    sweep_inner(grad_block, (POT, ADJ2))
    sent = []
    for plane in inner:
        for part in range(CHUNKS):
            sent.append((plane - 1) * CHUNKS + part)
            g_copy(sent[-1]).start()
    for part in parts:
        for plane, way in edges:
            wait_z(POT, way, part)
            wait_z(ADJ2, way, part)
            over_rows(part * chunk, chunk, lambda r: grad_block(plane, r))
            sent.append((plane - 1) * CHUNKS + part)
            g_copy(sent[-1]).start()
    for part in sent:
        plane, start = part // CHUNKS, (part % CHUNKS) * chunk
        at = pl.ds(start, chunk)
        g_copy(part).wait_recv()

    for part in sent:
        g_copy(part).wait_send()
    for way in (UP, DOWN):

        def z_done():
            z_copy(COND, way, 0).wait_send()
            for field in (ADJ0, POT, ADJ1, ADJ2):
                for part in range(CHUNKS):
                    z_copy(field, way, part).wait_send()

        def y_done():
            for field in range(5):
                y_copy(field, way).wait_send()

        guarded(z_has[way], z_done)
        guarded(y_has[way], y_done)


def local(counts, conductivity, receivers, observed, potential, adjoint_prev):
    planes, rows, lanes = conductivity.shape
    receivers = jnp.transpose(receivers, (1, 0, 2))
    wide = pltpu.VMEM((planes + 2, rows + 2 * PAD, lanes), jnp.float32)
    body = pltpu.VMEM((planes, rows, lanes), jnp.float32)
    dma = pltpu.SemaphoreType.DMA
    in_hbm = pl.BlockSpec(memory_space=pltpu.HBM)
    in_vmem = pl.BlockSpec(memory_space=pltpu.VMEM)
    adjoint, own, far = pl.pallas_call(
        functools.partial(kernel, counts),
        out_shape=(
            jax.ShapeDtypeStruct(adjoint_prev.shape, jnp.float32),
            jax.ShapeDtypeStruct(conductivity.shape, jnp.float32),
            jax.ShapeDtypeStruct(conductivity.shape, jnp.float32),
        ),
        in_specs=[in_hbm] * 5,
        out_specs=(in_vmem,) * 3,
        scratch_shapes=[wide] * 5
        + [body] * 2
        + [
            pltpu.VMEM(receivers.shape, jnp.int32),
            pltpu.VMEM(observed.shape, jnp.float32),
            dma((5,)),
            dma((5, 2, CHUNKS)),
            dma((5, 2, CHUNKS)),
            dma((5, 2)),
            dma((5, 2)),
            dma((2,)),
            dma((2,)),
            dma((planes * CHUNKS,)),
            dma((planes * CHUNKS,)),
        ],
        compiler_params=pltpu.CompilerParams(
            collective_id=0, has_side_effects=True, vmem_limit_bytes=VMEM_LIMIT
        ),
    )(
        *(
            pltpu.with_memory_space_constraint(x, pltpu.HBM)
            for x in (conductivity, receivers, observed, potential, adjoint_prev)
        )
    )
    return adjoint, own + far


def solution(mesh):
    counts = (mesh.shape["gz"], mesh.shape["gy"])
    return jax.shard_map(
        functools.partial(local, counts),
        mesh=mesh,
        in_specs=(
            P(("survey", "gz"), "gy", None),
            P(("survey", "pat"), None, None),
            P(("survey", "pat"), None),
            P("pat", ("survey", "gz"), "gy", None),
            P("pat", ("survey", "gz"), "gy", None),
        ),
        out_specs=(P("pat", ("survey", "gz"), "gy", None), P(("survey", "gz"), "gy", None)),
        check_vma=False,
    )
```

```python
import functools

import jax
import jax.numpy as jnp
from jax import lax
from jax.experimental import pallas as pl
from jax.experimental.pallas import tpu as pltpu
from jax.sharding import PartitionSpec as P

relax_weight = 0.8
MESH = pl.DeviceIdType.MESH
PAD = 8
UNROLLS = (4, 2, 1)
FINISH_LIMIT = 8 * 1024 * 1024
VMEM_LIMIT = 32 * 1024 * 1024
CHUNKS = 4
SPLIT = 4
COND, ADJ0, POT, ADJ1, ADJ2, FACE = range(6)
UP, DOWN = 0, 1
HIGH = lax.Precision.HIGHEST


def kernel(
    counts,
    cond_hbm,
    recv_hbm,
    obs_hbm,
    pot_hbm,
    adj_hbm,
    adj_out,
    grad,
    grad_far,
    cond,
    adj0,
    pot,
    adj1,
    adj2,
    source,
    weight,
    face,
    recv_ref,
    obs_ref,
    load_sem,
    z_send,
    z_recv,
    y_send,
    y_recv,
    relay_send,
    relay_recv,
    g_send,
    g_recv,
):
    gz_count, gy_count = counts
    planes, rows, lanes = cond_hbm.shape
    top = planes + 1
    chunk = rows // CHUNKS
    half = rows // 2
    gz = lax.axis_index("gz")
    gy = lax.axis_index("gy")
    pat = lax.axis_index("pat")
    partner = 1 - pat
    z_has = (gz < gz_count - 1, gz > 0)
    z_from = (gz > 0, gz < gz_count - 1)
    z_to = ({"gz": gz + 1}, {"gz": gz - 1})
    y_has = (gy < gy_count - 1, gy > 0)
    y_from = (gy > 0, gy < gy_count - 1)
    y_to = ({"gy": gy + 1}, {"gy": gy - 1})
    inside = pl.ds(PAD, rows)

    parts = [0, CHUNKS - 1] + list(range(1, CHUNKS - 1))

    def computes(way, part):
        turn = parts.index(part)
        return turn >= SPLIT or turn % 2 == way

    def moves(field, way, part):
        if field == COND:
            return part == 0
        if field in (POT, ADJ2):
            return computes(way, part)
        return field != FACE or not computes(way, part)

    hbm_of = {COND: cond_hbm, ADJ0: adj_hbm.at[0], POT: pot_hbm.at[0]}
    vmem_of = {COND: cond, ADJ0: adj0, POT: pot, ADJ1: adj1, ADJ2: adj2}

    loads = []
    for field in (COND, ADJ0, POT):
        loads.append(
            pltpu.make_async_copy(
                hbm_of[field], vmem_of[field].at[pl.ds(1, planes), inside], load_sem.at[field]
            )
        )
    loads.append(pltpu.make_async_copy(recv_hbm, recv_ref, load_sem.at[3]))
    loads.append(pltpu.make_async_copy(obs_hbm, obs_ref, load_sem.at[4]))
    for copy in loads:
        copy.start()

    barrier = pltpu.get_barrier_semaphore()
    for way in (UP, DOWN):

        @pl.when(z_has[way])
        def _():
            pl.semaphore_signal(barrier, inc=1, device_id=z_to[way], device_id_type=MESH)

        @pl.when(y_has[way])
        def _():
            pl.semaphore_signal(barrier, inc=1, device_id=y_to[way], device_id_type=MESH)

    pl.semaphore_signal(barrier, inc=1, device_id={"pat": partner}, device_id_type=MESH)

    for field in range(5):
        buf = vmem_of[field]
        for way in (UP, DOWN):

            @pl.when(jnp.logical_not(z_from[way]))
            def _():
                buf[0 if way == UP else top, PAD : PAD + rows] = jnp.zeros((rows, lanes), jnp.float32)

            @pl.when(jnp.logical_not(y_from[way]))
            def _():
                at = 0 if way == UP else PAD + rows
                buf[1:top, at : at + PAD] = jnp.zeros((planes, PAD, lanes), jnp.float32)

    neighbours = (
        1
        + z_has[0].astype(jnp.int32)
        + z_has[1].astype(jnp.int32)
        + y_has[0].astype(jnp.int32)
        + y_has[1].astype(jnp.int32)
    )
    pl.semaphore_wait(barrier, neighbours)

    def z_copy(field, way, part):
        if field == FACE:
            at = pl.ds(part * chunk, chunk)
            return pltpu.make_async_remote_copy(
                src_ref=face.at[1 - way, at],
                dst_ref=face.at[way, at],
                send_sem=z_send.at[field, way, part],
                recv_sem=z_recv.at[field, way, part],
                device_id=z_to[way],
                device_id_type=MESH,
            )
        buf = vmem_of[field]
        ghost = 0 if way == UP else top
        if field == COND:
            start, count = pl.multiple_of(pat * half, 8), half
        else:
            start, count = part * chunk, chunk
        if field in hbm_of:
            src = hbm_of[field].at[planes - 1 if way == UP else 0, pl.ds(start, count)]
        else:
            src = buf.at[planes if way == UP else 1, pl.ds(PAD + start, count)]
        return pltpu.make_async_remote_copy(
            src_ref=src,
            dst_ref=buf.at[ghost, pl.ds(PAD + start, count)],
            send_sem=z_send.at[field, way, part],
            recv_sem=z_recv.at[field, way, part],
            device_id=z_to[way],
            device_id_type=MESH,
        )

    def y_copy(field, way):
        buf = vmem_of[field]
        ghost = 0 if way == UP else PAD + rows
        if field in hbm_of:
            src = hbm_of[field].at[:, pl.ds(rows - PAD if way == UP else 0, PAD)]
        else:
            src = buf.at[pl.ds(1, planes), pl.ds(rows if way == UP else PAD, PAD)]
        return pltpu.make_async_remote_copy(
            src_ref=src,
            dst_ref=buf.at[pl.ds(1, planes), pl.ds(ghost, PAD)],
            send_sem=y_send.at[field, way],
            recv_sem=y_recv.at[field, way],
            device_id=y_to[way],
            device_id_type=MESH,
        )

    def relay(way):
        at = cond.at[0 if way == UP else top, pl.ds(pl.multiple_of(PAD + pat * half, 8), half)]
        return pltpu.make_async_remote_copy(
            src_ref=at,
            dst_ref=at,
            send_sem=relay_send.at[way],
            recv_sem=relay_recv.at[way],
            device_id={"pat": partner},
            device_id_type=MESH,
        )

    def g_copy(plane, part):
        if part is None:
            at, index = pl.ds(0, rows), 2 * CHUNKS + plane
        else:
            at, index = pl.ds(part * chunk, chunk), part + (CHUNKS if plane else 0)
        return pltpu.make_async_remote_copy(
            src_ref=grad.at[plane, at],
            dst_ref=grad_far.at[plane, at],
            send_sem=g_send.at[index],
            recv_sem=g_recv.at[index],
            device_id={"pat": partner},
            device_id_type=MESH,
        )

    def guarded(flag, action):
        @pl.when(flag)
        def _():
            action()

    def start_z(field, way, part):
        if not moves(field, way, part):
            return
        guarded(z_has[way], lambda: z_copy(field, way, part).start())

    def wait_z(field, way, part):
        if not moves(field, way, part):
            return
        guarded(z_from[way], lambda: z_copy(field, way, part).wait_recv())

    def start_y(field):
        for way in (UP, DOWN):
            guarded(y_has[way], lambda: y_copy(field, way).start())

    def wait_y(field):
        for way in (UP, DOWN):
            guarded(y_from[way], lambda: y_copy(field, way).wait_recv())

    for way in (UP, DOWN):
        start_z(COND, way, 0)
    for part in parts:
        for way in (UP, DOWN):
            start_z(ADJ0, way, part)
    for field in (COND, ADJ0, POT):
        start_y(field)

    for copy in loads:
        copy.wait()

    recv_count = recv_ref.shape[-1]
    z_at = recv_ref[0] - gz * planes
    y_at = recv_ref[1] - gy * rows
    near = (z_at >= 0) & (z_at < planes) & (y_at >= 0) & (y_at < rows)
    line = jnp.where(near, z_at * rows + y_at, -1)
    eye = lax.broadcasted_iota(jnp.int32, (recv_count, recv_count), 0) == lax.broadcasted_iota(
        jnp.int32, (recv_count, recv_count), 1
    )

    def column(row):
        wide = jnp.broadcast_to(row.astype(jnp.float32), (recv_count, recv_count))
        return jnp.sum(jnp.where(eye, wide, 0.0), axis=1, keepdims=True)

    line_col = column(line).astype(jnp.int32)
    x_col = column(recv_ref[2]).astype(jnp.int32)
    obs_col = column(obs_ref[...])
    picked = jnp.zeros((recv_count, lanes), jnp.float32)
    along = lax.broadcasted_iota(jnp.int32, (recv_count, rows), 1)
    for plane in range(planes):
        hot = jnp.where(along + plane * rows == line_col, 1.0, 0.0)
        picked = picked + jnp.dot(
            hot, pot[plane + 1, PAD : PAD + rows], precision=HIGH, preferred_element_type=jnp.float32
        )
    at_x = lax.broadcasted_iota(jnp.int32, (recv_count, lanes), 1) == x_col
    value = jnp.sum(jnp.where(at_x, picked, 0.0), axis=1, keepdims=True) - obs_col
    value = jnp.where(line_col >= 0, value, 0.0)
    spread = jnp.where(at_x, jnp.broadcast_to(value, at_x.shape), 0.0)
    down_rows = lax.broadcasted_iota(jnp.int32, (rows, recv_count), 0)
    for plane in range(planes):
        hot = jnp.where(down_rows + plane * rows == line, 1.0, 0.0)
        source[plane] = jnp.dot(hot, spread, precision=HIGH, preferred_element_type=jnp.float32)

    lane = lax.broadcasted_iota(jnp.int32, (8, lanes), 1)
    at_left = lane == 0
    at_right = lane == lanes - 1

    def left_of(v):
        return jnp.where(at_left, 0.0, pltpu.roll(v, 1, 1))

    def right_of(v):
        return jnp.where(at_right, 0.0, pltpu.roll(v, lanes - 1, 1))

    sub = lax.broadcasted_iota(jnp.int32, (8, lanes), 0)

    def beside(buf, plane, r, middle):
        before = buf[plane, pl.ds(pl.multiple_of(r - 8, 8), 8)]
        after = buf[plane, pl.ds(pl.multiple_of(r + 8, 8), 8)]
        return (
            pltpu.roll(jnp.where(sub == 7, before, middle), 1, 0),
            pltpu.roll(jnp.where(sub == 0, after, middle), 7, 0),
            buf[plane - 1, pl.ds(r, 8)],
            buf[plane + 1, pl.ds(r, 8)],
        )

    def relax_block(old, new, plane, r, first):
        c = cond[plane, pl.ds(r, 8)]
        a = old[plane, pl.ds(r, 8)]
        q = c * a
        sum_a = left_of(a) + right_of(a)
        sum_q = left_of(q) + right_of(q)
        if first:
            sum_c = left_of(c) + right_of(c)
        for c_n, a_n in zip(beside(cond, plane, r, c), beside(old, plane, r, a)):
            sum_a = sum_a + a_n
            sum_q = sum_q + c_n * a_n
            if first:
                sum_c = sum_c + c_n
        if first:
            diag = 3.0 * c + 0.5 * sum_c
            w = relax_weight / diag
            weight[plane - 1, pl.ds(pl.multiple_of(r - PAD, 8), 8)] = w
        else:
            w = weight[plane - 1, pl.ds(pl.multiple_of(r - PAD, 8), 8)]
        s = source[plane - 1, pl.ds(pl.multiple_of(r - PAD, 8), 8)]
        coupled = 0.5 * (c * sum_a + sum_q)
        value = (1.0 - relax_weight) * a + w * (s + coupled)
        new[plane, pl.ds(r, 8)] = value
        if not first:
            adj_out[0, plane - 1, pl.ds(pl.multiple_of(r - PAD, 8), 8)] = value

    def grad_block(plane, r):
        p = pot[plane, pl.ds(r, 8)]
        a = adj2[plane, pl.ds(r, 8)]
        total = (p - left_of(p)) * (a - left_of(a)) + (p - right_of(p)) * (a - right_of(a))
        pairs = list(zip(beside(pot, plane, r, p), beside(adj2, plane, r, a)))
        if plane == 1:
            del pairs[2]
        elif plane == planes:
            del pairs[3]
        for p_n, a_n in pairs:
            total = total + (p - p_n) * (a - a_n)
        grad[plane - 1, pl.ds(pl.multiple_of(r - PAD, 8), 8)] = -0.5 * total

    def face_block(plane, way, r):
        ghost = 0 if way == UP else top
        p = pot[plane, pl.ds(r, 8)] - pot[ghost, pl.ds(r, 8)]
        a = adj2[plane, pl.ds(r, 8)] - adj2[ghost, pl.ds(r, 8)]
        face[way, pl.ds(pl.multiple_of(r - PAD, 8), 8)] = p * a

    def close_block(plane, way, r):
        at = pl.ds(pl.multiple_of(r - PAD, 8), 8)
        grad[plane - 1, at] = grad[plane - 1, at] - 0.5 * face[way, at]

    def over_rows(first_row, count, action):
        blocks = count // 8
        step = next(n for n in UNROLLS if blocks % n == 0)

        def body(i, carry):
            for k in range(step):
                action(pl.multiple_of(PAD + first_row + (i * step + k) * 8, 8))
            return carry

        lax.fori_loop(0, blocks // step, body, 0)

    inner = list(range(2, planes))
    edges = [(1, UP), (planes, DOWN)]

    rims = [0, rows - 8]

    def sweep_inner(action, field):
        for plane in inner:
            over_rows(8, rows - 16, lambda r: action(plane, r))
        for each in field:
            wait_y(each)
        for plane in inner:
            for r in rims:
                action(plane, PAD + r)

    def first_block(plane, r):
        relax_block(adj0, adj1, plane, r, True)

    def second_block(plane, r):
        relax_block(adj1, adj2, plane, r, False)

    sweep_inner(first_block, (COND, ADJ0))
    for way in (UP, DOWN):

        def pass_on():
            z_copy(COND, way, 0).wait_recv()
            relay(way).start()

        guarded(z_from[way], pass_on)
    for way in (UP, DOWN):
        guarded(z_from[way], lambda: relay(way).wait())
    for i, part in enumerate(parts):
        for plane, way in edges:
            wait_z(ADJ0, way, part)
            over_rows(part * chunk, chunk, lambda r: first_block(plane, r))
            start_z(ADJ1, 1 - way, part)
        if i == min(1, CHUNKS - 1):
            start_y(ADJ1)
    for part in parts:
        for way in (UP, DOWN):
            start_z(POT, way, part)

    sweep_inner(second_block, (ADJ1,))
    for i, part in enumerate(parts):
        for plane, way in edges:
            wait_z(ADJ1, way, part)
            over_rows(part * chunk, chunk, lambda r: second_block(plane, r))
            start_z(ADJ2, 1 - way, part)
        if i == min(1, CHUNKS - 1):
            start_y(ADJ2)

    for plane in inner:
        over_rows(8, rows - 16, lambda r: grad_block(plane, r))
    for plane, way in edges:
        over_rows(8, rows - 16, lambda r: grad_block(plane, r))
    wait_y(POT)
    wait_y(ADJ2)
    for plane in inner + [1, planes]:
        for r in rims:
            grad_block(plane, PAD + r)
    sent = []

    def send_grad(plane, part):
        sent.append((plane, part))
        g_copy(plane, part).start()

    for plane in inner:
        send_grad(plane - 1, None)
    for part in parts:
        for plane, way in edges:

            def make_face():
                over_rows(part * chunk, chunk, lambda r: face_block(plane, way, r))

            if computes(way, part):
                wait_z(POT, way, part)
                wait_z(ADJ2, way, part)
                make_face()
                start_z(FACE, 1 - way, part)
            else:
                guarded(jnp.logical_not(z_from[way]), make_face)
    for part in parts[SPLIT:] + parts[:SPLIT]:
        for plane, way in edges:
            wait_z(FACE, way, part)
            over_rows(part * chunk, chunk, lambda r: close_block(plane, way, r))
            send_grad(plane - 1, part)
    for plane, part in sent:
        g_copy(plane, part).wait_recv()
    for plane, part in sent:
        g_copy(plane, part).wait_send()
    for way in (UP, DOWN):

        def z_done():
            z_copy(COND, way, 0).wait_send()
            for field in (ADJ0, POT, ADJ1, ADJ2, FACE):
                for part in range(CHUNKS):
                    if moves(field, way, part):
                        z_copy(field, way, part).wait_send()

        def y_done():
            for field in range(5):
                y_copy(field, way).wait_send()

        guarded(z_has[way], z_done)
        guarded(y_has[way], y_done)


def finish(adjoint, own, far, adj_out, grad_out, total, sems):
    planes = own.shape[0]
    copies = [pltpu.make_async_copy(adjoint, adj_out, sems.at[planes])]
    copies[0].start()
    for plane in range(planes):
        total[plane] = own[plane] + far[plane]
        copies.append(pltpu.make_async_copy(total.at[plane], grad_out.at[plane], sems.at[plane]))
        copies[-1].start()
    for copy in copies:
        copy.wait()


def local(counts, conductivity, receivers, observed, potential, adjoint_prev):
    planes, rows, lanes = conductivity.shape
    receivers = jnp.transpose(receivers, (1, 0, 2))
    wide = pltpu.VMEM((planes + 2, rows + 2 * PAD, lanes), jnp.float32)
    body = pltpu.VMEM((planes, rows, lanes), jnp.float32)
    dma = pltpu.SemaphoreType.DMA
    in_hbm = pl.BlockSpec(memory_space=pltpu.HBM)
    in_vmem = pl.BlockSpec(memory_space=pltpu.VMEM)
    adjoint, own, far = pl.pallas_call(
        functools.partial(kernel, counts),
        out_shape=(
            jax.ShapeDtypeStruct(adjoint_prev.shape, jnp.float32),
            jax.ShapeDtypeStruct(conductivity.shape, jnp.float32),
            jax.ShapeDtypeStruct(conductivity.shape, jnp.float32),
        ),
        in_specs=[in_hbm] * 5,
        out_specs=(in_vmem,) * 3,
        scratch_shapes=[wide] * 5
        + [body] * 2
        + [pltpu.VMEM((2, rows, lanes), jnp.float32)]
        + [
            pltpu.VMEM(receivers.shape, jnp.int32),
            pltpu.VMEM(observed.shape, jnp.float32),
            dma((5,)),
            dma((6, 2, CHUNKS)),
            dma((6, 2, CHUNKS)),
            dma((5, 2)),
            dma((5, 2)),
            dma((2,)),
            dma((2,)),
            dma((2 * CHUNKS + planes,)),
            dma((2 * CHUNKS + planes,)),
        ],
        compiler_params=pltpu.CompilerParams(
            collective_id=0, has_side_effects=True, vmem_limit_bytes=VMEM_LIMIT
        ),
    )(
        *(
            pltpu.with_memory_space_constraint(x, pltpu.HBM)
            for x in (conductivity, receivers, observed, potential, adjoint_prev)
        )
    )
    anywhere = pl.BlockSpec(memory_space=pl.ANY)
    return pl.pallas_call(
        finish,
        out_shape=(
            jax.ShapeDtypeStruct(adjoint.shape, jnp.float32),
            jax.ShapeDtypeStruct(own.shape, jnp.float32),
        ),
        in_specs=[in_vmem] * 3,
        out_specs=(anywhere, anywhere),
        scratch_shapes=[body, dma((planes + 1,))],
        compiler_params=pltpu.CompilerParams(vmem_limit_bytes=FINISH_LIMIT),
    )(adjoint, own, far)


def solution(mesh):
    counts = (mesh.shape["gz"], mesh.shape["gy"])
    return jax.shard_map(
        functools.partial(local, counts),
        mesh=mesh,
        in_specs=(
            P(("survey", "gz"), "gy", None),
            P(("survey", "pat"), None, None),
            P(("survey", "pat"), None),
            P("pat", ("survey", "gz"), "gy", None),
            P("pat", ("survey", "gz"), "gy", None),
        ),
        out_specs=(P("pat", ("survey", "gz"), "gy", None), P(("survey", "gz"), "gy", None)),
        check_vma=False,
    )
```
